128 devices in a mesh: dp: 32 (over y, x, core), chan: 4 (over z).
Axes of the slice: x: 4, y: 4, z: 4, core: 2. Of those that a mesh axis runs over, the one named last changes fastest.
Arguments:
- activations: bfloat16 [256, 32, 32, 512], P('dp'), may hold values from -12 to 12
- out_grads: bfloat16 [256, 32, 32, 512], P('dp', None, None, 'chan'), may hold values from -4 to 4
- weight: float32 [512, 3, 3, 512], P('dp', None, None, 'chan'), may hold values from -6 to 6
- momentum: float32 [512, 3, 3, 512], P('dp', None, None, 'chan'), may hold values from -6 to 6
Outputs:
- new_weight: float32 [512, 3, 3, 512], P('dp', None, None, 'chan')
- new_momentum: float32 [512, 3, 3, 512], P('dp', None, None, 'chan')
The draws below stay inside these ranges and needn't reach their ends.
All inputs are finite; a program needn't handle non-finite values.
Results may differ from the reference program's by a relative error of at most 0.0003.
Values sent between devices are 32-bit elements; how exact they have to be, the bound alone decides.
A program may use at most 64 MiB of HBM per device.

```python
import jax
import jax.numpy as jnp
from jax import lax

CIN = 512
COUT = 512
BATCH = 8
HEIGHT = 32
BREADTH = 32
REPLICAS = 32
N_CHAN = 4


def replica_scales(key_part):
    ramp = jnp.linspace(0.6, 1.8, REPLICAS)
    jitter = jnp.exp(jax.random.uniform(key_part, (REPLICAS,), minval=-0.22, maxval=0.22))
    return (ramp * jitter).reshape(REPLICAS, 1, 1, 1, 1)


def block_shares(key_part, blocks, width):
    ladder = jnp.linspace(0.35, 0.98, blocks).astype(jnp.float32)
    order = jax.random.permutation(key_part, blocks)
    return jnp.repeat(ladder[order], width // blocks)


def draw_activations(key, part):
    common = jax.random.normal(jax.random.fold_in(key, 11), (1, BATCH, HEIGHT, BREADTH, CIN))
    own = jax.random.normal(jax.random.fold_in(key, 12), (REPLICAS, BATCH, HEIGHT, BREADTH, CIN))
    shares = block_shares(jax.random.fold_in(key, 14), REPLICAS, CIN).reshape(1, 1, 1, 1, CIN)
    values = (shares * common + jnp.sqrt(1.0 - shares * shares) * own) * replica_scales(jax.random.fold_in(key, 13))
    values = jnp.clip(values, -12.0, 12.0)
    return values.reshape(REPLICAS * BATCH, HEIGHT, BREADTH, CIN).astype(jnp.bfloat16)


def draw_out_grads(key, part):
    common = jax.random.normal(jax.random.fold_in(key, 21), (1, BATCH, HEIGHT, BREADTH, COUT))
    own = jax.random.normal(jax.random.fold_in(key, 22), (REPLICAS, BATCH, HEIGHT, BREADTH, COUT))
    shares = block_shares(jax.random.fold_in(key, 25), N_CHAN, COUT).reshape(1, 1, 1, 1, COUT)
    channel_ramp = jnp.linspace(0.5, 1.5, COUT).reshape(1, 1, 1, 1, COUT)
    values = (shares * common + jnp.sqrt(1.0 - shares * shares) * own) * replica_scales(jax.random.fold_in(key, 23)) * channel_ramp
    values = values * (0.25 * (BATCH * HEIGHT * BREADTH) ** (-0.5)) * 16.0
    values = jnp.clip(values, -4.0, 4.0)
    return values.reshape(REPLICAS * BATCH, HEIGHT, BREADTH, COUT).astype(jnp.bfloat16)


def block_levels(stream_key, shape, pieces, least, largest):
    gain = 1.0
    for position, shards_of in pieces:
        draws = jax.random.uniform(jax.random.fold_in(jax.random.fold_in(stream_key, 6), position), (shards_of,), jnp.float32, least / len(pieces), largest / len(pieces))
        gain = gain * jnp.repeat(jnp.exp(draws), shape[position] // shards_of).reshape((-1,) + (1,) * (len(shape) - 1 - position))
    return gain


def noise(rng, extent, spread, limit, pieces=(), dtype=jnp.bfloat16):
    drawn = jax.random.normal(rng, extent, jnp.float32) * spread
    if len(pieces) > 0:
        drawn = block_levels(rng, extent, pieces, -0.22, 0.18) * drawn
    return jnp.clip(drawn, min=-limit, max=limit).astype(dtype)


def setup_inputs(seed: int = 0) -> dict:
    splits = jax.random.split(jax.random.key(seed), 5)
    activations = draw_activations(jax.random.fold_in(splits[4], 71), 0)
    out_grads = draw_out_grads(jax.random.fold_in(splits[4], 71), 0)
    weight = noise(splits[2], (CIN, 3, 3, COUT), 1.0, 6.0, ((0, 32), (3, 4)), jnp.float32)
    momentum = noise(splits[3], (CIN, 3, 3, COUT), 1.0, 6.0, ((0, 32), (3, 4)), jnp.float32)
    return {"activations": activations, "out_grads": out_grads, "weight": weight, "momentum": momentum}


def weight_gradient(pair):
    inputs, upstream = pair
    padded = jnp.pad(inputs, ((0, 0), (1, 1), (1, 1), (0, 0)))
    outputs = []
    for row_off in range(3):
        for col_off in range(3):
            window = padded[:, row_off:row_off + HEIGHT, col_off:col_off + BREADTH, :]
            outputs.append(jnp.einsum("bhwc,bhwo->co", window.astype(jnp.float32), upstream.astype(jnp.float32)))
    stacked = jnp.stack(outputs, axis=1)
    return stacked.reshape(CIN, 3, 3, COUT)


def combine(lower_vec, upper_vec):
    crossed = jnp.sum(lower_vec * upper_vec)
    lower_sq = jnp.sum(lower_vec * lower_vec) + 1e-6
    upper_sq = jnp.sum(upper_vec * upper_vec) + 1e-6
    return (1.0 - crossed / (2.0 * lower_sq)) * lower_vec + (1.0 - crossed / (2.0 * upper_sq)) * upper_vec


def reference(activations, out_grads, weight, momentum):
    inputs = activations.reshape(REPLICAS, BATCH, HEIGHT, BREADTH, CIN)
    upstream = out_grads.reshape(REPLICAS, BATCH, HEIGHT, BREADTH, COUT)
    gradients = lax.map(weight_gradient, (inputs, upstream))
    while gradients.shape[0] > 1:
        gradients = jax.vmap(combine)(gradients[0::2], gradients[1::2])
    adasum = gradients[0]
    new_momentum = 0.9 * momentum + adasum
    new_weight = weight - 0.1 * new_momentum
    return new_weight, new_momentum
```

```python
import jax
import jax.numpy as jnp
from jax import lax
from jax.experimental import pallas as pl
from jax.experimental.pallas import tpu as pltpu
from jax.sharding import PartitionSpec as P

MESH = pl.DeviceIdType.MESH
SIDE = 4
CHIPS = SIDE * SIDE
DEPTH = 4
ROWS = 16
LANES = 128
SAMPLES = 8
SPACE = 1024
CIN = 512
GROUPS = ((0, 4), (4, 9))
F32 = jnp.float32
EPS = 1e-6


def fold(block):
    halves = block[:, :8] + block[:, 8:]
    return jnp.sum(halves, axis=0)


def total(part):
    return jnp.sum(jnp.sum(part, axis=0, keepdims=True), axis=1, keepdims=True)


def shifted(sample):
    wide = sample.astype(F32)
    column = lax.broadcasted_iota(jnp.int32, wide.shape, 0) % 32
    left = jnp.where(column == 31, 0.0, pltpu.roll(wide, SPACE - 1, 0))
    right = jnp.where(column == 0, 0.0, pltpu.roll(wide, 1, 0))
    return left.astype(sample.dtype), sample, right.astype(sample.dtype)


def pair_weights(gram):
    row = lax.broadcasted_iota(jnp.int32, gram.shape, 0)
    col = lax.broadcasted_iota(jnp.int32, gram.shape, 1)
    weights = jnp.ones((CHIPS, 1), F32)
    size = 1
    while size < CHIPS:
        mine = row // size == col // size
        other = jnp.logical_and(row // (2 * size) == col // (2 * size), jnp.logical_not(mine))
        mask = mine.astype(F32)
        own = gram * mask
        cross = gram * other.astype(F32)
        own_c = jnp.sum(own, axis=0, keepdims=True)
        cross_c = jnp.sum(cross, axis=0, keepdims=True)
        own_r = jnp.sum(own, axis=1, keepdims=True)
        cross_r = jnp.sum(cross, axis=1, keepdims=True)
        square_r = jnp.sum(mask * own_c, axis=1, keepdims=True)
        inner_r = jnp.sum(mask * cross_c, axis=1, keepdims=True)
        square_c = jnp.sum(mask * own_r, axis=0, keepdims=True)
        inner_c = jnp.sum(mask * cross_r, axis=0, keepdims=True)
        coef_r = 1.0 - inner_r / (2.0 * (jnp.maximum(square_r, 0.0) + EPS))
        coef_c = 1.0 - inner_c / (2.0 * (jnp.maximum(square_c, 0.0) + EPS))
        gram = gram * coef_r * coef_c
        weights = weights * coef_r
        size *= 2
    return weights


def kernel(act_hbm, og_hbm, out_ref, act, og, pad, *rest):
    ngroups = len(GROUPS)
    grads, sibs, combs, recvs = (rest[ngroups * i : ngroups * (i + 1)] for i in range(4))
    (scal_src, scal, pairs, gram_src, gram_near, gram_mid, gram_far,
     load_sem, og_sem, sib_send, sib_recv, scal_send, scal_recv, comb_send, comb_recv,
     near_send, near_recv, far_send, far_recv) = rest[4 * ngroups :]

    dp = lax.axis_index("dp")
    z = lax.axis_index("chan")
    chip = dp // 2
    core = dp % 2
    y = chip // SIDE
    x = chip % SIDE
    slot = core * DEPTH + z

    def across(step):
        return (y + step // SIDE) % SIDE * SIDE + (x + step % SIDE) % SIDE

    def near(step):
        return (core + step // DEPTH) % 2, (z + step % DEPTH) % DEPTH

    for b in range(SAMPLES):
        pltpu.make_async_copy(act_hbm.at[b], act.at[b], load_sem.at[b]).start()
        pltpu.make_async_copy(og_hbm.at[b], og.at[b], og_sem.at[b]).start()

    barrier = pltpu.get_barrier_semaphore()

    def greet_far(step, carry):
        pl.semaphore_signal(barrier, inc=1, device_id={"dp": across(step) * 2 + core}, device_id_type=MESH)
        return carry

    def greet_near(step, carry):
        c2, z2 = near(step)
        pl.semaphore_signal(barrier, inc=1, device_id={"dp": chip * 2 + c2, "chan": z2}, device_id_type=MESH)
        return carry

    lax.fori_loop(1, CHIPS, greet_far, 0)
    lax.fori_loop(1, 2 * DEPTH, greet_near, 0)

    for g in grads:
        g[...] = jnp.zeros_like(g)
    pad[...] = jnp.zeros_like(pad)

    def accumulate(b, carry):
        pltpu.make_async_copy(act_hbm.at[b], act.at[b], load_sem.at[b]).wait()
        pltpu.make_async_copy(og_hbm.at[b], og.at[b], og_sem.at[b]).wait()
        for j, moved in enumerate(shifted(og[b])):
            pad[j, 32 : 32 + SPACE, :] = moved
        taps = jnp.concatenate(
            [pad[j, (2 - i) * 32 : (2 - i) * 32 + SPACE, :] for i in range(3) for j in range(3)], axis=1
        )
        product = lax.dot_general(act[b], taps, (((0,), (0,)), ((), ())), preferred_element_type=F32)
        for (first, last), g in zip(GROUPS, grads):
            for t in range(first, last):
                tap = product[:, t * LANES : (t + 1) * LANES].reshape(CHIPS, 2, ROWS, LANES)
                for half in range(2):
                    g[half, :, t - first] += tap[:, half]
        return carry

    lax.fori_loop(0, SAMPLES, accumulate, 0)

    pl.semaphore_wait(barrier, CHIPS - 1 + 2 * DEPTH - 1)

    swaps = []
    for n in range(ngroups):
        swap = pltpu.make_async_remote_copy(
            src_ref=grads[n].at[1 - core],
            dst_ref=sibs[n],
            send_sem=sib_send.at[n],
            recv_sem=sib_recv.at[n],
            device_id={"dp": chip * 2 + 1 - core},
            device_id_type=MESH,
        )
        swap.start()
        swaps.append(swap)
    zero = jnp.zeros((8, LANES), F32)
    sums = (zero, zero, zero)
    for n in range(ngroups):
        swaps[n].wait_recv()

        def products(q, carry, n=n):
            mine = grads[n][core, q]
            theirs = sibs[n][q]
            return (
                carry[0] + fold(mine * theirs),
                carry[1] + fold(mine * mine),
                carry[2] + fold(theirs * theirs),
            )

        sums = lax.fori_loop(0, CHIPS, products, sums)
    scal_src[0] = sums[0]
    scal_src[1] = jnp.where(core == 0, sums[1], sums[2])
    scal_src[2] = jnp.where(core == 0, sums[2], sums[1])
    scal[slot] = scal_src[...]

    def scal_copy(step):
        c2, z2 = near(step)
        return pltpu.make_async_remote_copy(
            src_ref=scal_src,
            dst_ref=scal.at[slot],
            send_sem=scal_send.at[step],
            recv_sem=scal_recv.at[slot],
            device_id={"dp": chip * 2 + c2, "chan": z2},
            device_id_type=MESH,
        )

    def near_wait(step, buffer, sem):
        c2, z2 = near(step)
        s2 = c2 * DEPTH + z2
        pltpu.make_async_copy(buffer.at[s2], buffer.at[s2], sem.at[s2]).wait()

    def start_scal(step, carry):
        scal_copy(step).start()
        return carry

    def wait_scal(step, carry):
        near_wait(step, scal, scal_recv)
        return carry

    lax.fori_loop(1, 2 * DEPTH, start_scal, 0)
    lax.fori_loop(1, 2 * DEPTH, wait_scal, 0)
    added = jnp.sum(scal[...], axis=0)
    inner, low_sq, high_sq = total(added[0]), total(added[1]), total(added[2])
    low = 1.0 - inner / (2.0 * (low_sq + EPS))
    high = 1.0 - inner / (2.0 * (high_sq + EPS))
    my_coef = jnp.where(core == 0, low, high)
    their_coef = jnp.where(core == 0, high, low)

    def comb_copy(n, step):
        q = across(step)
        return pltpu.make_async_remote_copy(
            src_ref=combs[n].at[q],
            dst_ref=recvs[n].at[chip],
            send_sem=comb_send.at[n, step],
            recv_sem=comb_recv.at[n, chip],
            device_id={"dp": q * 2 + core},
            device_id_type=MESH,
        )

    for n in range(ngroups):

        def send(step, carry, n=n):
            q = across(step)
            combs[n][q] = my_coef * grads[n][core, q] + their_coef * sibs[n][q]
            comb_copy(n, step).start()
            return carry

        lax.fori_loop(1, CHIPS, send, 0)
        recvs[n][chip] = my_coef * grads[n][core, chip] + their_coef * sibs[n][chip]

    for n in range(ngroups):

        def arrive(step, carry, n=n):
            q = across(step)
            pltpu.make_async_copy(recvs[n].at[q], recvs[n].at[q], comb_recv.at[n, q]).wait()
            return carry

        lax.fori_loop(1, CHIPS, arrive, 0)

        def against(s, carry, n=n):
            block = recvs[n][s]
            for t in range(CHIPS):
                part = fold(block * recvs[n][t])
                if n > 0:
                    part = part + pairs[s, t]
                pairs[s, t] = part
            return carry

        lax.fori_loop(0, CHIPS, against, 0)

    lane = lax.broadcasted_iota(jnp.int32, (CHIPS, LANES), 1)

    def collect(s, gram):
        column = jnp.sum(jnp.sum(pairs[s], axis=1), axis=1, keepdims=True)
        return gram + jnp.where(lane == s, column, 0.0)

    gram_src[...] = lax.fori_loop(0, CHIPS, collect, jnp.zeros((CHIPS, LANES), F32))

    gram_near[slot] = gram_src[...]

    def near_copy(step):
        c2, z2 = near(step)
        return pltpu.make_async_remote_copy(
            src_ref=gram_src,
            dst_ref=gram_near.at[slot],
            send_sem=near_send.at[step],
            recv_sem=near_recv.at[slot],
            device_id={"dp": chip * 2 + c2, "chan": z2},
            device_id_type=MESH,
        )

    def start_near(step, carry):
        near_copy(step).start()
        return carry

    def wait_near(step, carry):
        near_wait(step, gram_near, near_recv)
        return carry

    lax.fori_loop(1, 2 * DEPTH, start_near, 0)
    lax.fori_loop(1, 2 * DEPTH, wait_near, 0)
    gram_mid[...] = jnp.sum(gram_near[...], axis=0)
    gram_far[chip] = gram_mid[...]

    def far_copy(step):
        return pltpu.make_async_remote_copy(
            src_ref=gram_mid,
            dst_ref=gram_far.at[chip],
            send_sem=far_send.at[step],
            recv_sem=far_recv.at[chip],
            device_id={"dp": across(step) * 2 + core},
            device_id_type=MESH,
        )

    def start_far(step, carry):
        far_copy(step).start()
        return carry

    def wait_far(step, carry):
        q = across(step)
        pltpu.make_async_copy(gram_far.at[q], gram_far.at[q], far_recv.at[q]).wait()
        return carry

    lax.fori_loop(1, CHIPS, start_far, 0)
    lax.fori_loop(1, CHIPS, wait_far, 0)
    weights = pair_weights(jnp.sum(gram_far[...], axis=0))

    for (first, last), block in zip(GROUPS, recvs):
        for t in range(first, last):
            tap = weights[0:1] * block[0, t - first]
            for s in range(1, CHIPS):
                tap = tap + weights[s : s + 1] * block[s, t - first]
            out_ref[t] = tap

    for n in range(ngroups):
        swaps[n].wait_send()

    def near_left(step, carry):
        scal_copy(step).wait_send()
        near_copy(step).wait_send()
        return carry

    def far_left(step, carry):
        for n in range(ngroups):
            comb_copy(n, step).wait_send()
        far_copy(step).wait_send()
        return carry

    lax.fori_loop(1, 2 * DEPTH, near_left, 0)
    lax.fori_loop(1, CHIPS, far_left, 0)


def adasum(activations, out_grads):
    bf16 = jnp.bfloat16
    widths = [last - first for first, last in GROUPS]
    ngroups = len(GROUPS)
    scratch = [
        pltpu.VMEM((SAMPLES, SPACE, CIN), bf16),
        pltpu.VMEM((SAMPLES, SPACE, LANES), bf16),
        pltpu.VMEM((3, SPACE + 64, LANES), bf16),
    ]
    scratch += [pltpu.VMEM((2, CHIPS, w, ROWS, LANES), F32) for w in widths]
    scratch += [pltpu.VMEM((CHIPS, w, ROWS, LANES), F32) for _ in range(3) for w in widths]
    scratch += [
        pltpu.VMEM((3, 8, LANES), F32),
        pltpu.VMEM((2 * DEPTH, 3, 8, LANES), F32),
        pltpu.VMEM((CHIPS, CHIPS, 8, LANES), F32),
        pltpu.VMEM((CHIPS, LANES), F32),
        pltpu.VMEM((2 * DEPTH, CHIPS, LANES), F32),
        pltpu.VMEM((CHIPS, LANES), F32),
        pltpu.VMEM((CHIPS, CHIPS, LANES), F32),
    ]
    scratch += [
        pltpu.SemaphoreType.DMA(shape)
        for shape in (
            (SAMPLES,), (SAMPLES,), (ngroups,), (ngroups,), (2 * DEPTH,), (2 * DEPTH,),
            (ngroups, CHIPS), (ngroups, CHIPS), (2 * DEPTH,), (2 * DEPTH,), (CHIPS,), (CHIPS,),
        )
    ]
    return pl.pallas_call(
        kernel,
        out_shape=jax.ShapeDtypeStruct((9, ROWS, LANES), F32),
        in_specs=[pl.BlockSpec(memory_space=pl.ANY)] * 2,
        out_specs=pl.BlockSpec(memory_space=pltpu.VMEM),
        scratch_shapes=scratch,
        compiler_params=pltpu.CompilerParams(
            collective_id=0, has_side_effects=True, vmem_limit_bytes=62 << 20
        ),
        name="adasum",
    )(activations.reshape(SAMPLES, SPACE, CIN), out_grads.reshape(SAMPLES, SPACE, LANES))


def shards(activations, out_grads, weight, momentum):
    combined = adasum(activations, out_grads)
    combined = combined.transpose(1, 0, 2).reshape(weight.shape)
    new_momentum = 0.9 * momentum + combined
    new_weight = weight - 0.1 * new_momentum
    return new_weight, new_momentum


def solution(mesh):
    in_specs = (
        P("dp", None, None, None),
        P("dp", None, None, "chan"),
        P("dp", None, None, "chan"),
        P("dp", None, None, "chan"),
    )
    out_specs = (P("dp", None, None, "chan"), P("dp", None, None, "chan"))
    return jax.shard_map(shards, mesh=mesh, in_specs=in_specs, out_specs=out_specs, check_vma=False)
```

```python
import jax
import jax.numpy as jnp
from jax import lax
from jax.experimental import pallas as pl
from jax.experimental.pallas import tpu as pltpu
from jax.sharding import PartitionSpec as P

MESH = pl.DeviceIdType.MESH
SIDE = 4
CHIPS = SIDE * SIDE
DEPTH = 4
ROWS = 16
LANES = 128
SAMPLES = 8
SPACE = 1024
CIN = 512
TAPS = 9
EARLY = 4
MIDDLE = 7
F32 = jnp.float32
EPS = 1e-6


def fold(block):
    halves = block[:, :8] + block[:, 8:]
    return jnp.sum(halves, axis=0)


def total(part):
    return jnp.sum(jnp.sum(part, axis=0, keepdims=True), axis=1, keepdims=True)


def shifted(sample):
    wide = sample.astype(F32)
    column = lax.broadcasted_iota(jnp.int32, wide.shape, 0) % 32
    left = jnp.where(column == 31, 0.0, pltpu.roll(wide, SPACE - 1, 0))
    right = jnp.where(column == 0, 0.0, pltpu.roll(wide, 1, 0))
    return left.astype(sample.dtype), sample, right.astype(sample.dtype)


def pair_weights(gram):
    row = lax.broadcasted_iota(jnp.int32, gram.shape, 0)
    col = lax.broadcasted_iota(jnp.int32, gram.shape, 1)
    weights = jnp.ones((CHIPS, 1), F32)
    size = 1
    while size < CHIPS:
        mine = row // size == col // size
        other = jnp.logical_and(row // (2 * size) == col // (2 * size), jnp.logical_not(mine))
        mask = mine.astype(F32)
        own = gram * mask
        cross = gram * other.astype(F32)
        own_c = jnp.sum(own, axis=0, keepdims=True)
        cross_c = jnp.sum(cross, axis=0, keepdims=True)
        own_r = jnp.sum(own, axis=1, keepdims=True)
        cross_r = jnp.sum(cross, axis=1, keepdims=True)
        square_r = jnp.sum(mask * own_c, axis=1, keepdims=True)
        inner_r = jnp.sum(mask * cross_c, axis=1, keepdims=True)
        square_c = jnp.sum(mask * own_r, axis=0, keepdims=True)
        inner_c = jnp.sum(mask * cross_r, axis=0, keepdims=True)
        coef_r = 1.0 - inner_r / (2.0 * (jnp.maximum(square_r, 0.0) + EPS))
        coef_c = 1.0 - inner_c / (2.0 * (jnp.maximum(square_c, 0.0) + EPS))
        gram = gram * coef_r * coef_c
        weights = weights * coef_r
        size *= 2
    return weights


def kernel(act_hbm, og_hbm, out_ref, act, og, pad, grad_a, grad_b, grad_c, sib_a, sib_b, sib_c, raw, comb, block_a, block_b,
           scal_src, scal, coef_src, coef, pairs, gram_src, gram_near, gram_mid, gram_far,
           load_sem, og_sem, sib_send, sib_recv, raw_send, raw_recv, scal_send, scal_recv, coef_send, coef_recv,
           comb_send, comb_recv, near_send, near_recv, far_send, far_recv):
    dp = lax.axis_index("dp")
    z = lax.axis_index("chan")
    chip = dp // 2
    core = dp - chip * 2
    y = chip // SIDE
    x = chip - y * SIDE
    slot = core * DEPTH + z

    def wrap(value):
        return jnp.where(value >= SIDE, value - SIDE, value)

    rows_at = [y] + [wrap(y + d) * SIDE for d in range(SIDE)][1:]
    rows_at[0] = y * SIDE
    cols_at = [x] + [wrap(x + d) for d in range(1, SIDE)]
    chips = [rows_at[k // SIDE] + cols_at[k % SIDE] for k in range(1, CHIPS)]
    deep = [z] + [wrap(z + d) for d in range(1, DEPTH)]
    mates = [(core if k < DEPTH else 1 - core, deep[k % DEPTH]) for k in range(1, 2 * DEPTH)]

    for b in range(SAMPLES):
        pltpu.make_async_copy(og_hbm.at[b], og.at[b], og_sem.at[b]).start()
        pltpu.make_async_copy(act_hbm.at[b], act.at[b], load_sem.at[b]).start()

    barrier = pltpu.get_barrier_semaphore()
    for q in chips:
        pl.semaphore_signal(barrier, inc=1, device_id={"dp": q * 2 + core}, device_id_type=MESH)
        pl.semaphore_signal(barrier, inc=1, device_id={"dp": q * 2 + 1 - core}, device_id_type=MESH)
    for c2, z2 in mates:
        pl.semaphore_signal(barrier, inc=1, device_id={"dp": chip * 2 + c2, "chan": z2}, device_id_type=MESH)

    def remote(src, dst, send, recv, dp_to, z_to=None):
        to = {"dp": dp_to} if z_to is None else {"dp": dp_to, "chan": z_to}
        return pltpu.make_async_remote_copy(
            src_ref=src, dst_ref=dst, send_sem=send, recv_sem=recv, device_id=to, device_id_type=MESH
        )

    def landed(ref, sem):
        pltpu.make_async_copy(ref, ref, sem).wait()

    for j in range(3):
        for b in range(SAMPLES):
            pad[j, b, :32] = jnp.zeros((32, LANES), pad.dtype)
            pad[j, b, 32 + SPACE :] = jnp.zeros((32, LANES), pad.dtype)

    def columns(b, taps):
        return jnp.concatenate(
            [pad[t % 3, b, (2 - t // 3) * 32 : (2 - t // 3) * 32 + SPACE, :] for t in taps], axis=1
        )

    def store(grad, product, first):
        for t in range(product.shape[1] // LANES):
            tap = product[:, t * LANES : (t + 1) * LANES].reshape(CHIPS, 2, ROWS, LANES)
            for half in range(2):
                if first:
                    grad[half, :, t] = tap[:, half]
                else:
                    grad[half, :, t] += tap[:, half]

    def product(left, right):
        return lax.dot_general(left, right, (((0,), (0,)), ((), ())), preferred_element_type=F32)

    def move(b):
        for j, moved in enumerate(shifted(og[b])):
            pad[j, b, 32 : 32 + SPACE, :] = moved

    def early(b, carry, first=False, last=False):
        landed(act.at[b], load_sem.at[b])
        if not last:
            landed(og.at[b + 1], og_sem.at[b + 1])
        store(grad_a, product(act[b], columns(b, range(EARLY))), first)
        if not last:
            move(b + 1)
        return carry

    def later(grad, taps, span):
        def body(k, carry, first=False):
            left = act[pl.ds(span * k, span)].reshape(span * SPACE, CIN)
            right = jnp.concatenate([columns(span * k + n, taps) for n in range(span)], axis=0)
            store(grad, product(left, right), first)
            return carry

        body(0, 0, True)
        lax.fori_loop(1, SAMPLES // span, body, 0)

    landed(og.at[0], og_sem.at[0])
    move(0)
    early(0, 0, first=True)
    lax.fori_loop(1, SAMPLES - 1, early, 0)
    early(SAMPLES - 1, 0, last=True)

    pl.semaphore_wait(barrier, 2 * (CHIPS - 1) + 2 * DEPTH - 1)

    def swap(n, grad, sib):
        copy = remote(grad.at[1 - core], sib, sib_send.at[n], sib_recv.at[n], chip * 2 + 1 - core)
        copy.start()
        return copy

    swaps = [swap(0, grad_a, sib_a)]
    for q in chips:
        for half in range(2):
            remote(
                grad_a.at[half, q], raw.at[core, chip], raw_send.at[half], raw_recv.at[core], q * 2 + half
            ).start()

    later(grad_b, range(EARLY, MIDDLE), 2)
    swaps.append(swap(1, grad_b, sib_b))
    later(grad_c, range(MIDDLE, TAPS), 4)
    swaps.append(swap(2, grad_c, sib_c))

    def products(grad, sib, sums):
        def body(q, carry):
            mine = grad[core, q]
            theirs = sib[q]
            return (
                carry[0] + fold(mine * theirs),
                carry[1] + fold(mine * mine),
                carry[2] + fold(theirs * theirs),
            )

        return lax.fori_loop(0, CHIPS, body, sums)

    zero = jnp.zeros((8, LANES), F32)
    sums = (zero, zero, zero)
    for copy, grad, sib in zip(swaps, (grad_a, grad_b, grad_c), (sib_a, sib_b, sib_c)):
        copy.wait_recv()
        sums = products(grad, sib, sums)
    scal_src[0] = sums[0]
    scal_src[1] = jnp.where(core == 0, sums[1], sums[2])
    scal_src[2] = jnp.where(core == 0, sums[2], sums[1])
    for c2, z2 in mates:
        remote(scal_src, scal.at[slot], scal_send.at[0], scal_recv.at[0], chip * 2 + c2, z2).start()
    scal[slot] = scal_src[...]
    landed(scal.at[: 2 * DEPTH - 1], scal_recv.at[0])
    added = jnp.sum(scal[...], axis=0)
    inner, low_sq, high_sq = total(added[0]), total(added[1]), total(added[2])
    low = 1.0 - inner / (2.0 * (low_sq + EPS))
    high = 1.0 - inner / (2.0 * (high_sq + EPS))
    coef_src[0:1] = jnp.broadcast_to(low, (1, LANES))
    coef_src[1:2] = jnp.broadcast_to(high, (1, LANES))
    my_coef = jnp.where(core == 0, low, high)
    their_coef = jnp.where(core == 0, high, low)

    wide = MIDDLE - EARLY
    for k, q in enumerate(chips):
        remote(coef_src, coef.at[chip], coef_send.at[0], coef_recv.at[0], q * 2 + core).start()
        comb[k, :wide] = my_coef * grad_b[core, q] + their_coef * sib_b[q]
        comb[k, wide:] = my_coef * grad_c[core, q] + their_coef * sib_c[q]
        remote(comb.at[k], block_b.at[chip], comb_send.at[0], comb_recv.at[0], q * 2 + core).start()
    block_b[chip, :wide] = my_coef * grad_b[core, chip] + their_coef * sib_b[chip]
    block_b[chip, wide:] = my_coef * grad_c[core, chip] + their_coef * sib_c[chip]
    block_a[chip] = my_coef * grad_a[core, chip] + their_coef * sib_a[chip]
    for half in range(2):
        landed(raw.at[half, : CHIPS - 1], raw_recv.at[half])
    landed(coef.at[: CHIPS - 1], coef_recv.at[0])
    for q in chips:
        block_a[q] = coef[q, 0:1] * raw[0, q] + coef[q, 1:2] * raw[1, q]

    def against(block, more):
        def body(s, carry):
            mine = block[s]
            for t in range(CHIPS):
                part = fold(mine * block[t])
                pairs[s, t] = part + pairs[s, t] if more else part
            return carry

        lax.fori_loop(0, CHIPS, body, 0)

    against(block_a, False)
    landed(block_b.at[: CHIPS - 1], comb_recv.at[0])
    against(block_b, True)

    sums = jnp.sum(jnp.sum(pairs[...].reshape(CHIPS * CHIPS, 8, LANES), axis=1), axis=1, keepdims=True)
    index = lax.broadcasted_iota(jnp.int32, (CHIPS * CHIPS, LANES), 0)
    lane = lax.broadcasted_iota(jnp.int32, (CHIPS * CHIPS, LANES), 1)
    spread = jnp.where(lane == index // CHIPS, sums, 0.0)
    gram_src[...] = jnp.sum(spread.reshape(CHIPS, CHIPS, LANES), axis=0)

    for c2, z2 in mates:
        remote(gram_src, gram_near.at[slot], near_send.at[0], near_recv.at[0], chip * 2 + c2, z2).start()
    gram_near[slot] = gram_src[...]
    for copy in swaps:
        copy.wait_send()
    for half in range(2):
        landed(raw.at[half, : CHIPS - 1], raw_send.at[half])
    landed(scal.at[: 2 * DEPTH - 1], scal_send.at[0])
    landed(coef.at[: CHIPS - 1], coef_send.at[0])
    landed(comb, comb_send.at[0])
    landed(gram_near.at[: 2 * DEPTH - 1], near_recv.at[0])
    gram_mid[...] = jnp.sum(gram_near[...], axis=0)
    for q in chips:
        remote(gram_mid, gram_far.at[chip], far_send.at[0], far_recv.at[0], q * 2 + core).start()
    gram_far[chip] = gram_mid[...]
    landed(gram_near.at[: 2 * DEPTH - 1], near_send.at[0])
    landed(gram_far.at[: CHIPS - 1], far_recv.at[0])
    weights = pair_weights(jnp.sum(gram_far[...], axis=0))

    for t in range(TAPS):
        block, u = (block_a, t) if t < EARLY else (block_b, t - EARLY)
        tap = weights[0:1] * block[0, u]
        for s in range(1, CHIPS):
            tap = tap + weights[s : s + 1] * block[s, u]
        out_ref[t] = tap
    landed(gram_far.at[: CHIPS - 1], far_send.at[0])


def adasum(activations, out_grads):
    bf16 = jnp.bfloat16
    late = TAPS - EARLY
    scratch = [
        pltpu.VMEM((SAMPLES, SPACE, CIN), bf16),
        pltpu.VMEM((SAMPLES, SPACE, LANES), bf16),
        pltpu.VMEM((3, SAMPLES, SPACE + 64, LANES), bf16),
    ]
    scratch += [
        pltpu.VMEM(shape, F32)
        for shape in (
            (2, CHIPS, EARLY, ROWS, LANES),
            (2, CHIPS, MIDDLE - EARLY, ROWS, LANES),
            (2, CHIPS, TAPS - MIDDLE, ROWS, LANES),
            (CHIPS, EARLY, ROWS, LANES),
            (CHIPS, MIDDLE - EARLY, ROWS, LANES),
            (CHIPS, TAPS - MIDDLE, ROWS, LANES),
            (2, CHIPS, EARLY, ROWS, LANES),
            (CHIPS - 1, late, ROWS, LANES),
            (CHIPS, EARLY, ROWS, LANES),
            (CHIPS, late, ROWS, LANES),
            (3, 8, LANES),
            (2 * DEPTH, 3, 8, LANES),
            (2, LANES),
            (CHIPS, 2, LANES),
            (CHIPS, CHIPS, 8, LANES),
            (CHIPS, LANES),
            (2 * DEPTH, CHIPS, LANES),
            (CHIPS, LANES),
            (CHIPS, CHIPS, LANES),
        )
    ]
    scratch += [
        pltpu.SemaphoreType.DMA(shape)
        for shape in (
            (SAMPLES,), (SAMPLES,), (3,), (3,), (2,), (2,), (1,), (1,), (1,), (1,), (1,), (1,), (1,), (1,), (1,), (1,),
        )
    ]
    return pl.pallas_call(
        kernel,
        out_shape=jax.ShapeDtypeStruct((9, ROWS, LANES), F32),
        in_specs=[pl.BlockSpec(memory_space=pltpu.HBM)] * 2,
        out_specs=pl.BlockSpec(memory_space=pltpu.VMEM),
        scratch_shapes=scratch,
        compiler_params=pltpu.CompilerParams(
            collective_id=0, has_side_effects=True, vmem_limit_bytes=52 << 20
        ),
        name="adasum",
    )(activations.reshape(SAMPLES, SPACE, CIN), out_grads.reshape(SAMPLES, SPACE, LANES))


def shards(activations, out_grads, weight, momentum):
    combined = adasum(activations, out_grads)
    combined = combined.transpose(1, 0, 2).reshape(weight.shape)
    new_momentum = 0.9 * momentum + combined
    new_weight = weight - 0.1 * new_momentum
    return new_weight, new_momentum


def solution(mesh):
    in_specs = (
        P("dp", None, None, None),
        P("dp", None, None, "chan"),
        P("dp", None, None, "chan"),
        P("dp", None, None, "chan"),
    )
    out_specs = (P("dp", None, None, "chan"), P("dp", None, None, "chan"))
    return jax.shard_map(shards, mesh=mesh, in_specs=in_specs, out_specs=out_specs, check_vma=False)
```

```python
import jax
import jax.numpy as jnp
from jax import lax
from jax.experimental import pallas as pl
from jax.experimental.pallas import tpu as pltpu
from jax.sharding import PartitionSpec as P

MESH = pl.DeviceIdType.MESH
SIDE = 4
CHIPS = SIDE * SIDE
DEPTH = 4
ROWS = 16
LANES = 128
SAMPLES = 8
SPACE = 1024
CIN = 512
TAPS = 9
EARLY = 4
MIDDLE = 7
F32 = jnp.float32
EPS = 1e-6
ROUTE = (
    (2, 2), (0, 1), (2, 1), (1, 0), (1, 2), (0, 3), (2, 3), (3, 0), (3, 2), (1, 1), (2, 0), (3, 3), (0, 2), (1, 3), (3, 1),
)
PACKED = 8


def hops(step):
    return sum(min(d, SIDE - d) for d in (step[0], step[1], step[3]))


EVERYONE = sorted(
    [(dy, dx, dc, dz) for dy in range(SIDE) for dx in range(SIDE) for dc in range(2) for dz in range(DEPTH)][1:],
    key=lambda step: -hops(step),
)
DEVICES = len(EVERYONE) + 1


def fold(block):
    halves = block[:, :8] + block[:, 8:]
    return jnp.sum(halves, axis=0)


def total(part):
    return jnp.sum(jnp.sum(part, axis=0, keepdims=True), axis=1, keepdims=True)


def shifted(sample):
    wide = sample.astype(F32)
    column = lax.broadcasted_iota(jnp.int32, wide.shape, 0) % 32
    left = jnp.where(column == 31, 0.0, pltpu.roll(wide, SPACE - 1, 0))
    right = jnp.where(column == 0, 0.0, pltpu.roll(wide, 1, 0))
    return left.astype(sample.dtype), sample, right.astype(sample.dtype)


def pair_weights(gram):
    row = lax.broadcasted_iota(jnp.int32, gram.shape, 0)
    col = lax.broadcasted_iota(jnp.int32, gram.shape, 1)
    weights = jnp.ones((CHIPS, 1), F32)
    size = 1
    while size < CHIPS:
        mine = row // size == col // size
        other = jnp.logical_and(row // (2 * size) == col // (2 * size), jnp.logical_not(mine))
        mask = mine.astype(F32)
        own = gram * mask
        cross = gram * other.astype(F32)
        own_c = jnp.sum(own, axis=0, keepdims=True)
        cross_c = jnp.sum(cross, axis=0, keepdims=True)
        own_r = jnp.sum(own, axis=1, keepdims=True)
        cross_r = jnp.sum(cross, axis=1, keepdims=True)
        square_r = jnp.sum(mask * own_c, axis=1, keepdims=True)
        inner_r = jnp.sum(mask * cross_c, axis=1, keepdims=True)
        square_c = jnp.sum(mask * own_r, axis=0, keepdims=True)
        inner_c = jnp.sum(mask * cross_r, axis=0, keepdims=True)
        coef_r = 1.0 - inner_r / (2.0 * (jnp.maximum(square_r, 0.0) + EPS))
        coef_c = 1.0 - inner_c / (2.0 * (jnp.maximum(square_c, 0.0) + EPS))
        gram = gram * coef_r * coef_c
        weights = weights * coef_r
        size *= 2
    return weights


def kernel(act_hbm, og_hbm, out_ref, act, og, pad, grad_a, grad_b, grad_c, sib_a, sib_b, sib_c, raw, comb, block_a, block_b,
           scal_src, scal, coef_src, coef, pairs, gram_src, gram_all,
           load_sem, og_sem, sib_send, sib_recv, raw_send, raw_recv, scal_send, scal_recv, coef_send, coef_recv,
           comb_send, comb_recv, gram_send, gram_recv):
    dp = lax.axis_index("dp")
    z = lax.axis_index("chan")
    chip = dp // 2
    core = dp - chip * 2
    y = chip // SIDE
    x = chip - y * SIDE
    slot = core * DEPTH + z

    def wrap(value):
        return jnp.where(value >= SIDE, value - SIDE, value)

    rows_at = [y] + [wrap(y + d) * SIDE for d in range(SIDE)][1:]
    rows_at[0] = y * SIDE
    cols_at = [x] + [wrap(x + d) for d in range(1, SIDE)]
    chips = [rows_at[dy] + cols_at[dx] for dy, dx in ROUTE]
    deep = [z] + [wrap(z + d) for d in range(1, DEPTH)]
    mates = [(core if k < DEPTH else 1 - core, deep[k % DEPTH]) for k in range(1, 2 * DEPTH)]

    for b in range(SAMPLES):
        pltpu.make_async_copy(og_hbm.at[b], og.at[b], og_sem.at[b]).start()
        pltpu.make_async_copy(act_hbm.at[b], act.at[b], load_sem.at[b]).start()

    barrier = pltpu.get_barrier_semaphore()
    everyone = [
        (rows_at[dy] * 2 + cols_at[dx] * 2 + (1 - core if dc else core), deep[dz]) for dy, dx, dc, dz in EVERYONE
    ]
    for device, level in everyone:
        pl.semaphore_signal(barrier, inc=1, device_id={"dp": device, "chan": level}, device_id_type=MESH)

    def remote(src, dst, send, recv, dp_to, z_to=None):
        to = {"dp": dp_to} if z_to is None else {"dp": dp_to, "chan": z_to}
        return pltpu.make_async_remote_copy(
            src_ref=src, dst_ref=dst, send_sem=send, recv_sem=recv, device_id=to, device_id_type=MESH
        )

    def landed(ref, sem):
        pltpu.make_async_copy(ref, ref, sem).wait()

    for j in range(3):
        for b in range(SAMPLES):
            pad[j, b, :32] = jnp.zeros((32, LANES), pad.dtype)
            pad[j, b, 32 + SPACE :] = jnp.zeros((32, LANES), pad.dtype)

    def columns(b, taps):
        return jnp.concatenate(
            [pad[t % 3, b, (2 - t // 3) * 32 : (2 - t // 3) * 32 + SPACE, :] for t in taps], axis=1
        )

    def store(grad, product, first):
        for t in range(product.shape[1] // LANES):
            tap = product[:, t * LANES : (t + 1) * LANES].reshape(CHIPS, 2, ROWS, LANES)
            for half in range(2):
                if first:
                    grad[half, :, t] = tap[:, half]
                else:
                    grad[half, :, t] += tap[:, half]

    def product(left, right):
        return lax.dot_general(left, right, (((0,), (0,)), ((), ())), preferred_element_type=F32)

    def move(b):
        for j, moved in enumerate(shifted(og[b])):
            pad[j, b, 32 : 32 + SPACE, :] = moved

    def early(b, carry, first=False, last=False):
        landed(act.at[b], load_sem.at[b])
        if not last:
            landed(og.at[b + 1], og_sem.at[b + 1])
        store(grad_a, product(act[b], columns(b, range(EARLY))), first)
        if not last:
            move(b + 1)
        return carry

    def later(grad, taps, span):
        def body(k, carry, first=False):
            left = act[pl.ds(span * k, span)].reshape(span * SPACE, CIN)
            right = jnp.concatenate([columns(span * k + n, taps) for n in range(span)], axis=0)
            store(grad, product(left, right), first)
            return carry

        body(0, 0, True)
        lax.fori_loop(1, SAMPLES // span, body, 0)

    landed(og.at[0], og_sem.at[0])
    move(0)
    early(0, 0, first=True)
    lax.fori_loop(1, SAMPLES - 1, early, 0)
    early(SAMPLES - 1, 0, last=True)

    pl.semaphore_wait(barrier, DEVICES - 1)

    def swap(n, grad, sib):
        copy = remote(grad.at[1 - core], sib, sib_send.at[n], sib_recv.at[n], chip * 2 + 1 - core)
        copy.start()
        return copy

    swaps = [swap(0, grad_a, sib_a)]
    for q in chips:
        for half in range(2):
            remote(
                grad_a.at[half, q], raw.at[core, chip], raw_send.at[half], raw_recv.at[core], q * 2 + half
            ).start()

    later(grad_b, range(EARLY, MIDDLE), 2)
    swaps.append(swap(1, grad_b, sib_b))
    later(grad_c, range(MIDDLE, TAPS), 4)
    swaps.append(swap(2, grad_c, sib_c))

    def products(grad, sib, sums):
        def body(q, carry):
            mine = grad[core, q]
            theirs = sib[q]
            return (
                carry[0] + fold(mine * theirs),
                carry[1] + fold(mine * mine),
                carry[2] + fold(theirs * theirs),
            )

        return lax.fori_loop(0, CHIPS, body, sums)

    zero = jnp.zeros((8, LANES), F32)
    sums = (zero, zero, zero)
    for copy, grad, sib in zip(swaps, (grad_a, grad_b, grad_c), (sib_a, sib_b, sib_c)):
        copy.wait_recv()
        sums = products(grad, sib, sums)
    scal_src[0] = sums[0]
    scal_src[1] = jnp.where(core == 0, sums[1], sums[2])
    scal_src[2] = jnp.where(core == 0, sums[2], sums[1])
    for c2, z2 in mates:
        remote(scal_src, scal.at[slot], scal_send.at[0], scal_recv.at[0], chip * 2 + c2, z2).start()
    scal[slot] = scal_src[...]
    landed(scal.at[: 2 * DEPTH - 1], scal_recv.at[0])
    added = jnp.sum(scal[...], axis=0)
    inner, low_sq, high_sq = total(added[0]), total(added[1]), total(added[2])
    low = 1.0 - inner / (2.0 * (low_sq + EPS))
    high = 1.0 - inner / (2.0 * (high_sq + EPS))
    coef_src[0:1] = jnp.broadcast_to(low, (1, LANES))
    coef_src[1:2] = jnp.broadcast_to(high, (1, LANES))
    my_coef = jnp.where(core == 0, low, high)
    their_coef = jnp.where(core == 0, high, low)

    wide = MIDDLE - EARLY
    for k, q in enumerate(chips):
        remote(coef_src, coef.at[chip], coef_send.at[0], coef_recv.at[0], q * 2 + core).start()
        comb[k, :wide] = my_coef * grad_b[core, q] + their_coef * sib_b[q]
        comb[k, wide:] = my_coef * grad_c[core, q] + their_coef * sib_c[q]
        remote(comb.at[k], block_b.at[chip], comb_send.at[0], comb_recv.at[0], q * 2 + core).start()
    block_b[chip, :wide] = my_coef * grad_b[core, chip] + their_coef * sib_b[chip]
    block_b[chip, wide:] = my_coef * grad_c[core, chip] + their_coef * sib_c[chip]
    block_a[chip] = my_coef * grad_a[core, chip] + their_coef * sib_a[chip]
    for half in range(2):
        landed(raw.at[half, : CHIPS - 1], raw_recv.at[half])
    landed(coef.at[: CHIPS - 1], coef_recv.at[0])
    for q in chips:
        block_a[q] = coef[q, 0:1] * raw[0, q] + coef[q, 1:2] * raw[1, q]

    def against(block, more):
        def body(s, carry):
            mine = block[s]
            for t in range(CHIPS):
                part = fold(mine * block[t])
                pairs[s, t] = part + pairs[s, t] if more else part
            return carry

        lax.fori_loop(0, CHIPS, body, 0)

    against(block_a, False)
    landed(block_b.at[: CHIPS - 1], comb_recv.at[0])
    against(block_b, True)

    sums = jnp.sum(jnp.sum(pairs[...].reshape(CHIPS * CHIPS, 8, LANES), axis=1), axis=1, keepdims=True)
    index = lax.broadcasted_iota(jnp.int32, (CHIPS * CHIPS, LANES), 0)
    lane = lax.broadcasted_iota(jnp.int32, (CHIPS * CHIPS, LANES), 1)
    spread = jnp.where(lane == index % (CHIPS * PACKED), sums, 0.0)
    gram_src[...] = jnp.sum(spread.reshape(2, CHIPS * PACKED, LANES), axis=1)

    here = dp * DEPTH + z
    for device, level in everyone:
        remote(gram_src, gram_all.at[here], gram_send.at[0], gram_recv.at[0], device, level).start()
    gram_all[here] = gram_src[...]
    for copy in swaps:
        copy.wait_send()
    for half in range(2):
        landed(raw.at[half, : CHIPS - 1], raw_send.at[half])
    landed(scal.at[: 2 * DEPTH - 1], scal_send.at[0])
    landed(coef.at[: CHIPS - 1], coef_send.at[0])
    landed(comb, comb_send.at[0])
    landed(gram_all.at[: DEVICES - 1], gram_recv.at[0])
    packed = jnp.sum(gram_all[...], axis=0)
    rows = jnp.concatenate([jnp.broadcast_to(packed[n : n + 1], (PACKED, LANES)) for n in range(2)], axis=0)
    row = lax.broadcasted_iota(jnp.int32, (CHIPS, LANES), 0) % PACKED
    gram = rows
    for n in range(1, PACKED):
        gram = jnp.where(row == n, pltpu.roll(rows, LANES - CHIPS * n, 1), gram)
    gram = jnp.where(lax.broadcasted_iota(jnp.int32, (CHIPS, LANES), 1) < CHIPS, gram, 0.0)
    weights = pair_weights(gram)

    for t in range(TAPS):
        block, u = (block_a, t) if t < EARLY else (block_b, t - EARLY)
        tap = weights[0:1] * block[0, u]
        for s in range(1, CHIPS):
            tap = tap + weights[s : s + 1] * block[s, u]
        out_ref[t] = tap
    landed(gram_all.at[: DEVICES - 1], gram_send.at[0])


def adasum(activations, out_grads):
    bf16 = jnp.bfloat16
    late = TAPS - EARLY
    scratch = [
        pltpu.VMEM((SAMPLES, SPACE, CIN), bf16),
        pltpu.VMEM((SAMPLES, SPACE, LANES), bf16),
        pltpu.VMEM((3, SAMPLES, SPACE + 64, LANES), bf16),
    ]
    scratch += [
        pltpu.VMEM(shape, F32)
        for shape in (
            (2, CHIPS, EARLY, ROWS, LANES),
            (2, CHIPS, MIDDLE - EARLY, ROWS, LANES),
            (2, CHIPS, TAPS - MIDDLE, ROWS, LANES),
            (CHIPS, EARLY, ROWS, LANES),
            (CHIPS, MIDDLE - EARLY, ROWS, LANES),
            (CHIPS, TAPS - MIDDLE, ROWS, LANES),
            (2, CHIPS, EARLY, ROWS, LANES),
            (CHIPS - 1, late, ROWS, LANES),
            (CHIPS, EARLY, ROWS, LANES),
            (CHIPS, late, ROWS, LANES),
            (3, 8, LANES),
            (2 * DEPTH, 3, 8, LANES),
            (2, LANES),
            (CHIPS, 2, LANES),
            (CHIPS, CHIPS, 8, LANES),
            (2, LANES),
            (DEVICES, 2, LANES),
        )
    ]
    scratch += [
        pltpu.SemaphoreType.DMA(shape)
        for shape in (
            (SAMPLES,), (SAMPLES,), (3,), (3,), (2,), (2,), (1,), (1,), (1,), (1,), (1,), (1,), (1,), (1,),
        )
    ]
    return pl.pallas_call(
        kernel,
        out_shape=jax.ShapeDtypeStruct((9, ROWS, LANES), F32),
        in_specs=[pl.BlockSpec(memory_space=pltpu.HBM)] * 2,
        out_specs=pl.BlockSpec(memory_space=pltpu.VMEM),
        scratch_shapes=scratch,
        compiler_params=pltpu.CompilerParams(
            collective_id=0, has_side_effects=True, vmem_limit_bytes=52 << 20
        ),
        name="adasum",
    )(activations.reshape(SAMPLES, SPACE, CIN), out_grads.reshape(SAMPLES, SPACE, LANES))


def shards(activations, out_grads, weight, momentum):
    combined = adasum(activations, out_grads)
    combined = combined.transpose(1, 0, 2).reshape(weight.shape)
    new_momentum = 0.9 * momentum + combined
    new_weight = weight - 0.1 * new_momentum
    return new_weight, new_momentum


def solution(mesh):
    in_specs = (
        P("dp", None, None, None),
        P("dp", None, None, "chan"),
        P("dp", None, None, "chan"),
        P("dp", None, None, "chan"),
    )
    out_specs = (P("dp", None, None, "chan"), P("dp", None, None, "chan"))
    return jax.shard_map(shards, mesh=mesh, in_specs=in_specs, out_specs=out_specs, check_vma=False)
```

```python
import jax
import jax.numpy as jnp
from jax import lax
from jax.experimental import pallas as pl
from jax.experimental.pallas import tpu as pltpu
from jax.sharding import PartitionSpec as P

MESH = pl.DeviceIdType.MESH
SIDE = 4
CHIPS = SIDE * SIDE
DEPTH = 4
ROWS = 16
LANES = 128
SAMPLES = 8
SPACE = 1024
CIN = 512
TAPS = 9
EARLY = 4
MIDDLE = 8
RAW = 5
F32 = jnp.float32
EPS = 1e-6
ROUTE = (
    (2, 2), (0, 1), (2, 1), (1, 0), (1, 2), (0, 3), (2, 3), (3, 0), (3, 2), (1, 1), (2, 0), (3, 3), (0, 2), (1, 3), (3, 1),
)
PACKED = 8


def hops(step):
    return sum(min(d, SIDE - d) for d in (step[0], step[1], step[3]))


EVERYONE = sorted(
    [(dy, dx, dc, dz) for dy in range(SIDE) for dx in range(SIDE) for dc in range(2) for dz in range(DEPTH)][1:],
    key=lambda step: -hops(step),
)
DEVICES = len(EVERYONE) + 1


def fold(block):
    halves = block[:, :8] + block[:, 8:]
    return jnp.sum(halves, axis=0)


def total(part):
    return jnp.sum(jnp.sum(part, axis=0, keepdims=True), axis=1, keepdims=True)


def shifted(sample):
    wide = sample.astype(F32)
    column = lax.broadcasted_iota(jnp.int32, wide.shape, 0) % 32
    left = jnp.where(column == 31, 0.0, pltpu.roll(wide, SPACE - 1, 0))
    right = jnp.where(column == 0, 0.0, pltpu.roll(wide, 1, 0))
    return left.astype(sample.dtype), sample, right.astype(sample.dtype)


def pair_weights(gram):
    row = lax.broadcasted_iota(jnp.int32, gram.shape, 0)
    col = lax.broadcasted_iota(jnp.int32, gram.shape, 1)
    weights = jnp.ones((CHIPS, 1), F32)
    size = 1
    while size < CHIPS:
        mine = row // size == col // size
        other = jnp.logical_and(row // (2 * size) == col // (2 * size), jnp.logical_not(mine))
        mask = mine.astype(F32)
        own = gram * mask
        cross = gram * other.astype(F32)
        own_c = jnp.sum(own, axis=0, keepdims=True)
        cross_c = jnp.sum(cross, axis=0, keepdims=True)
        own_r = jnp.sum(own, axis=1, keepdims=True)
        cross_r = jnp.sum(cross, axis=1, keepdims=True)
        square_r = jnp.sum(mask * own_c, axis=1, keepdims=True)
        inner_r = jnp.sum(mask * cross_c, axis=1, keepdims=True)
        square_c = jnp.sum(mask * own_r, axis=0, keepdims=True)
        inner_c = jnp.sum(mask * cross_r, axis=0, keepdims=True)
        coef_r = 1.0 - inner_r / (2.0 * (jnp.maximum(square_r, 0.0) + EPS))
        coef_c = 1.0 - inner_c / (2.0 * (jnp.maximum(square_c, 0.0) + EPS))
        gram = gram * coef_r * coef_c
        weights = weights * coef_r
        size *= 2
    return weights


def kernel(act_hbm, og_hbm, out_ref, act, og, pad, grad_a, grad_b, grad_c, sib_a, sib_b, sib_c, raw_a, raw_b, comb_b, comb_c, block_a, block_b, block_c,
           scal_src, scal, coef_src, coef, pairs, gram_src, gram_all,
           load_sem, og_sem, sib_send, sib_recv, raw_send, raw_recv, scal_send, scal_recv, coef_send, coef_recv,
           comb_send, comb_recv, gram_send, gram_recv):
    dp = lax.axis_index("dp")
    z = lax.axis_index("chan")
    chip = dp // 2
    core = dp - chip * 2
    y = chip // SIDE
    x = chip - y * SIDE
    slot = core * DEPTH + z

    def wrap(value):
        return jnp.where(value >= SIDE, value - SIDE, value)

    rows_at = [y] + [wrap(y + d) * SIDE for d in range(SIDE)][1:]
    rows_at[0] = y * SIDE
    cols_at = [x] + [wrap(x + d) for d in range(1, SIDE)]
    chips = [rows_at[dy] + cols_at[dx] for dy, dx in ROUTE]
    deep = [z] + [wrap(z + d) for d in range(1, DEPTH)]
    mates = [(core if k < DEPTH else 1 - core, deep[k % DEPTH]) for k in range(1, 2 * DEPTH)]

    for b in range(SAMPLES):
        pltpu.make_async_copy(og_hbm.at[b], og.at[b], og_sem.at[b]).start()
        pltpu.make_async_copy(act_hbm.at[b], act.at[b], load_sem.at[b]).start()

    barrier = pltpu.get_barrier_semaphore()
    everyone = [
        (rows_at[dy] * 2 + cols_at[dx] * 2 + (1 - core if dc else core), deep[dz]) for dy, dx, dc, dz in EVERYONE
    ]
    for q in chips:
        for half in range(2):
            pl.semaphore_signal(barrier, inc=1, device_id={"dp": q * 2 + half}, device_id_type=MESH)
    for c2, z2 in mates:
        pl.semaphore_signal(barrier, inc=1, device_id={"dp": chip * 2 + c2, "chan": z2}, device_id_type=MESH)

    def remote(src, dst, send, recv, dp_to, z_to=None):
        to = {"dp": dp_to} if z_to is None else {"dp": dp_to, "chan": z_to}
        return pltpu.make_async_remote_copy(
            src_ref=src, dst_ref=dst, send_sem=send, recv_sem=recv, device_id=to, device_id_type=MESH
        )

    def landed(ref, sem):
        pltpu.make_async_copy(ref, ref, sem).wait()

    for j in range(3):
        for b in range(SAMPLES):
            pad[j, b, :32] = jnp.zeros((32, LANES), pad.dtype)
            pad[j, b, 32 + SPACE :] = jnp.zeros((32, LANES), pad.dtype)

    def columns(b, taps):
        return jnp.concatenate(
            [pad[t % 3, b, (2 - t // 3) * 32 : (2 - t // 3) * 32 + SPACE, :] for t in taps], axis=1
        )

    def store(grad, product, first):
        for t in range(product.shape[1] // LANES):
            tap = product[:, t * LANES : (t + 1) * LANES].reshape(CHIPS, 2, ROWS, LANES)
            for half in range(2):
                if first:
                    grad[half, :, t] = tap[:, half]
                else:
                    grad[half, :, t] += tap[:, half]

    def product(left, right):
        return lax.dot_general(left, right, (((0,), (0,)), ((), ())), preferred_element_type=F32)

    def move(b):
        for j, moved in enumerate(shifted(og[b])):
            pad[j, b, 32 : 32 + SPACE, :] = moved

    def early(b, carry, first=False, last=False):
        landed(act.at[b], load_sem.at[b])
        if not last:
            landed(og.at[b + 1], og_sem.at[b + 1])
        store(grad_a, product(act[b], columns(b, range(EARLY))), first)
        if not last:
            move(b + 1)
        return carry

    def later(grad, taps, span):
        def body(k, carry, first=False):
            left = act[pl.ds(span * k, span)].reshape(span * SPACE, CIN)
            right = jnp.concatenate([columns(span * k + n, taps) for n in range(span)], axis=0)
            store(grad, product(left, right), first)
            return carry

        body(0, 0, True)
        lax.fori_loop(1, SAMPLES // span, body, 0)

    landed(og.at[0], og_sem.at[0])
    move(0)
    early(0, 0, first=True)
    lax.fori_loop(1, SAMPLES - 1, early, 0)
    early(SAMPLES - 1, 0, last=True)

    pl.semaphore_wait(barrier, 2 * (CHIPS - 1) + 2 * DEPTH - 1)

    def swap(n, grad, sib):
        copy = remote(grad.at[1 - core], sib, sib_send.at[n], sib_recv.at[n], chip * 2 + 1 - core)
        copy.start()
        return copy

    swaps = [swap(0, grad_a, sib_a)]
    for q in chips:
        for half in range(2):
            remote(
                grad_a.at[half, q], raw_a.at[core, chip], raw_send.at[half], raw_recv.at[core], q * 2 + half
            ).start()

    later(grad_b, range(EARLY, MIDDLE), 2)
    swaps.append(swap(1, grad_b, sib_b))
    for q in chips:
        for half in range(2):
            remote(
                grad_b.at[half, q, : RAW - EARLY],
                raw_b.at[core, chip],
                raw_send.at[2 + half],
                raw_recv.at[2 + core],
                q * 2 + half,
            ).start()
    later(grad_c, range(MIDDLE, TAPS), 4)
    swaps.append(swap(2, grad_c, sib_c))

    def products(grad, sib, sums):
        def body(q, carry):
            mine = grad[core, q]
            theirs = sib[q]
            return (
                carry[0] + fold(mine * theirs),
                carry[1] + fold(mine * mine),
                carry[2] + fold(theirs * theirs),
            )

        return lax.fori_loop(0, CHIPS, body, sums, unroll=4)

    zero = jnp.zeros((8, LANES), F32)
    sums = (zero, zero, zero)
    for copy, grad, sib in zip(swaps, (grad_a, grad_b, grad_c), (sib_a, sib_b, sib_c)):
        copy.wait_recv()
        sums = products(grad, sib, sums)
    scal_src[0] = sums[0]
    scal_src[1] = jnp.where(core == 0, sums[1], sums[2])
    scal_src[2] = jnp.where(core == 0, sums[2], sums[1])
    for c2, z2 in mates:
        remote(scal_src, scal.at[slot], scal_send.at[0], scal_recv.at[0], chip * 2 + c2, z2).start()
    scal[slot] = scal_src[...]
    landed(scal.at[: 2 * DEPTH - 1], scal_recv.at[0])
    added = jnp.sum(scal[...], axis=0)
    inner, low_sq, high_sq = total(added[0]), total(added[1]), total(added[2])
    low = 1.0 - inner / (2.0 * (low_sq + EPS))
    high = 1.0 - inner / (2.0 * (high_sq + EPS))
    coef_src[0:1] = jnp.broadcast_to(low, (1, LANES))
    coef_src[1:2] = jnp.broadcast_to(high, (1, LANES))
    my_coef = jnp.where(core == 0, low, high)
    their_coef = jnp.where(core == 0, high, low)

    skip = RAW - EARLY

    def mixed(mine, theirs):
        return my_coef * mine + their_coef * theirs

    for k, q in enumerate(chips):
        remote(coef_src, coef.at[chip], coef_send.at[0], coef_recv.at[0], q * 2 + core).start()
        comb_b[k] = mixed(grad_b[core, q, skip:], sib_b[q, skip:])
        remote(comb_b.at[k], block_b.at[chip], comb_send.at[0], comb_recv.at[0], q * 2 + core).start()
    for k, q in enumerate(chips):
        comb_c[k] = mixed(grad_c[core, q], sib_c[q])
        remote(comb_c.at[k], block_c.at[chip], comb_send.at[1], comb_recv.at[1], q * 2 + core).start()
    block_b[chip] = mixed(grad_b[core, chip, skip:], sib_b[chip, skip:])
    block_c[chip] = mixed(grad_c[core, chip], sib_c[chip])
    block_a[chip, :EARLY] = my_coef * grad_a[core, chip] + their_coef * sib_a[chip]
    block_a[chip, EARLY:] = my_coef * grad_b[core, chip, :skip] + their_coef * sib_b[chip, :skip]
    for half in range(2):
        landed(raw_a.at[half, : CHIPS - 1], raw_recv.at[half])
        landed(raw_b.at[half, : CHIPS - 1], raw_recv.at[2 + half])
    landed(coef.at[: CHIPS - 1], coef_recv.at[0])
    for q in chips:
        block_a[q, :EARLY] = coef[q, 0:1] * raw_a[0, q] + coef[q, 1:2] * raw_a[1, q]
        block_a[q, EARLY:] = coef[q, 0:1] * raw_b[0, q] + coef[q, 1:2] * raw_b[1, q]

    def against(block, more):
        def body(s, carry):
            mine = block[s]
            for t in range(CHIPS):
                part = fold(mine * block[t])
                pairs[s, t] = part + pairs[s, t] if more else part
            return carry

        lax.fori_loop(0, CHIPS, body, 0)

    against(block_a, False)
    landed(block_b.at[: CHIPS - 1], comb_recv.at[0])
    against(block_b, True)
    landed(block_c.at[: CHIPS - 1], comb_recv.at[1])
    against(block_c, True)

    sums = jnp.sum(jnp.sum(pairs[...].reshape(CHIPS * CHIPS, 8, LANES), axis=1), axis=1, keepdims=True)
    index = lax.broadcasted_iota(jnp.int32, (CHIPS * CHIPS, LANES), 0)
    lane = lax.broadcasted_iota(jnp.int32, (CHIPS * CHIPS, LANES), 1)
    spread = jnp.where(lane == index % (CHIPS * PACKED), sums, 0.0)
    gram_src[...] = jnp.sum(spread.reshape(2, CHIPS * PACKED, LANES), axis=1)

    here = dp * DEPTH + z
    for device, level in everyone:
        remote(gram_src, gram_all.at[here], gram_send.at[0], gram_recv.at[0], device, level).start()
    gram_all[here] = gram_src[...]
    for copy in swaps:
        copy.wait_send()
    for half in range(2):
        landed(raw_a.at[half, : CHIPS - 1], raw_send.at[half])
        landed(raw_b.at[half, : CHIPS - 1], raw_send.at[2 + half])
    landed(scal.at[: 2 * DEPTH - 1], scal_send.at[0])
    landed(coef.at[: CHIPS - 1], coef_send.at[0])
    landed(comb_b, comb_send.at[0])
    landed(comb_c, comb_send.at[1])
    landed(gram_all.at[: DEVICES - 1], gram_recv.at[0])
    packed = jnp.sum(gram_all[...], axis=0)
    rows = jnp.concatenate([jnp.broadcast_to(packed[n : n + 1], (PACKED, LANES)) for n in range(2)], axis=0)
    row = lax.broadcasted_iota(jnp.int32, (CHIPS, LANES), 0) % PACKED
    gram = rows
    for n in range(1, PACKED):
        gram = jnp.where(row == n, pltpu.roll(rows, LANES - CHIPS * n, 1), gram)
    gram = jnp.where(lax.broadcasted_iota(jnp.int32, (CHIPS, LANES), 1) < CHIPS, gram, 0.0)
    weights = pair_weights(gram)

    for t in range(TAPS):
        block, u = (block_a, t) if t < RAW else (block_b, t - RAW) if t < MIDDLE else (block_c, t - MIDDLE)
        tap = weights[0:1] * block[0, u]
        for s in range(1, CHIPS):
            tap = tap + weights[s : s + 1] * block[s, u]
        out_ref[t] = tap
    landed(gram_all.at[: DEVICES - 1], gram_send.at[0])


def adasum(activations, out_grads):
    bf16 = jnp.bfloat16
    scratch = [
        pltpu.VMEM((SAMPLES, SPACE, CIN), bf16),
        pltpu.VMEM((SAMPLES, SPACE, LANES), bf16),
        pltpu.VMEM((3, SAMPLES, SPACE + 64, LANES), bf16),
    ]
    scratch += [
        pltpu.VMEM(shape, F32)
        for shape in (
            (2, CHIPS, EARLY, ROWS, LANES),
            (2, CHIPS, MIDDLE - EARLY, ROWS, LANES),
            (2, CHIPS, TAPS - MIDDLE, ROWS, LANES),
            (CHIPS, EARLY, ROWS, LANES),
            (CHIPS, MIDDLE - EARLY, ROWS, LANES),
            (CHIPS, TAPS - MIDDLE, ROWS, LANES),
            (2, CHIPS, EARLY, ROWS, LANES),
            (2, CHIPS, RAW - EARLY, ROWS, LANES),
            (CHIPS - 1, MIDDLE - RAW, ROWS, LANES),
            (CHIPS - 1, TAPS - MIDDLE, ROWS, LANES),
            (CHIPS, RAW, ROWS, LANES),
            (CHIPS, MIDDLE - RAW, ROWS, LANES),
            (CHIPS, TAPS - MIDDLE, ROWS, LANES),
            (3, 8, LANES),
            (2 * DEPTH, 3, 8, LANES),
            (2, LANES),
            (CHIPS, 2, LANES),
            (CHIPS, CHIPS, 8, LANES),
            (2, LANES),
            (DEVICES, 2, LANES),
        )
    ]
    scratch += [
        pltpu.SemaphoreType.DMA(shape)
        for shape in (
            (SAMPLES,), (SAMPLES,), (3,), (3,), (4,), (4,), (1,), (1,), (1,), (1,), (2,), (2,), (1,), (1,),
        )
    ]
    return pl.pallas_call(
        kernel,
        out_shape=jax.ShapeDtypeStruct((9, ROWS, LANES), F32),
        in_specs=[pl.BlockSpec(memory_space=pltpu.HBM)] * 2,
        out_specs=pl.BlockSpec(memory_space=pltpu.VMEM),
        scratch_shapes=scratch,
        compiler_params=pltpu.CompilerParams(
            collective_id=0, has_side_effects=True, vmem_limit_bytes=52 << 20
        ),
        name="adasum",
    )(activations.reshape(SAMPLES, SPACE, CIN), out_grads.reshape(SAMPLES, SPACE, LANES))


def shards(activations, out_grads, weight, momentum):
    combined = adasum(activations, out_grads)
    combined = combined.transpose(1, 0, 2).reshape(weight.shape)
    new_momentum = 0.9 * momentum + combined
    new_weight = weight - 0.1 * new_momentum
    return new_weight, new_momentum


def solution(mesh):
    in_specs = (
        P("dp", None, None, None),
        P("dp", None, None, "chan"),
        P("dp", None, None, "chan"),
        P("dp", None, None, "chan"),
    )
    out_specs = (P("dp", None, None, "chan"), P("dp", None, None, "chan"))
    return jax.shard_map(shards, mesh=mesh, in_specs=in_specs, out_specs=out_specs, check_vma=False)
```

```python
import jax
import jax.numpy as jnp
from jax import lax
from jax.experimental import pallas as pl
from jax.experimental.pallas import tpu as pltpu
from jax.sharding import PartitionSpec as P

MESH = pl.DeviceIdType.MESH
SIDE = 4
CHIPS = SIDE * SIDE
DEPTH = 4
ROWS = 16
LANES = 128
SAMPLES = 8
SPACE = 1024
CIN = 512
TAPS = 9
EARLY = 4
MIDDLE = 8
RAW = 5
F32 = jnp.float32
EPS = 1e-6
ROUTE = (
    (2, 2), (0, 1), (2, 1), (1, 0), (1, 2), (0, 3), (2, 3), (3, 0), (3, 2), (1, 1), (2, 0), (3, 3), (0, 2), (1, 3), (3, 1),
)
PACKED = 8


def hops(step):
    return sum(min(d, SIDE - d) for d in (step[0], step[1], step[3]))


EVERYONE = sorted(
    [(dy, dx, dc, dz) for dy in range(SIDE) for dx in range(SIDE) for dc in range(2) for dz in range(DEPTH)][1:],
    key=lambda step: -hops(step),
)
DEVICES = len(EVERYONE) + 1


def fold(block):
    halves = block[:, :8] + block[:, 8:]
    return jnp.sum(halves, axis=0)


def total(part):
    return jnp.sum(jnp.sum(part, axis=0, keepdims=True), axis=1, keepdims=True)


def shifted(sample):
    wide = sample.astype(F32)
    column = lax.broadcasted_iota(jnp.int32, wide.shape, 0) % 32
    left = jnp.where(column == 31, 0.0, pltpu.roll(wide, SPACE - 1, 0))
    right = jnp.where(column == 0, 0.0, pltpu.roll(wide, 1, 0))
    return left.astype(sample.dtype), sample, right.astype(sample.dtype)


def pair_weights(gram):
    row = lax.broadcasted_iota(jnp.int32, gram.shape, 0)
    col = lax.broadcasted_iota(jnp.int32, gram.shape, 1)
    weights = jnp.ones((CHIPS, 1), F32)
    size = 1
    while size < CHIPS:
        mine = row // size == col // size
        other = jnp.logical_and(row // (2 * size) == col // (2 * size), jnp.logical_not(mine))
        mask = mine.astype(F32)
        own = gram * mask
        cross = gram * other.astype(F32)
        own_c = jnp.sum(own, axis=0, keepdims=True)
        cross_c = jnp.sum(cross, axis=0, keepdims=True)
        own_r = jnp.sum(own, axis=1, keepdims=True)
        cross_r = jnp.sum(cross, axis=1, keepdims=True)
        square_r = jnp.sum(mask * own_c, axis=1, keepdims=True)
        inner_r = jnp.sum(mask * cross_c, axis=1, keepdims=True)
        square_c = jnp.sum(mask * own_r, axis=0, keepdims=True)
        inner_c = jnp.sum(mask * cross_r, axis=0, keepdims=True)
        coef_r = 1.0 - inner_r / (2.0 * (jnp.maximum(square_r, 0.0) + EPS))
        coef_c = 1.0 - inner_c / (2.0 * (jnp.maximum(square_c, 0.0) + EPS))
        gram = gram * coef_r * coef_c
        weights = weights * coef_r
        size *= 2
    return weights


def kernel(act_hbm, og_hbm, out_ref, act, og, pad, grad_a, grad_b, grad_c, sib_a, sib_b, sib_c, raw_a, raw_b, comb_b, comb_c, block_a, block_b, block_c,
           scal_src, scal, coef_src, coef, pairs, gram_src, gram_all,
           load_sem, og_sem, sib_send, sib_recv, raw_send, raw_recv, scal_send, scal_recv, coef_send, coef_recv,
           comb_send, comb_recv, gram_send, gram_recv):
    dp = lax.axis_index("dp")
    z = lax.axis_index("chan")
    chip = dp // 2
    core = dp - chip * 2
    y = chip // SIDE
    x = chip - y * SIDE
    slot = core * DEPTH + z

    def wrap(value):
        return jnp.where(value >= SIDE, value - SIDE, value)

    rows_at = [y] + [wrap(y + d) * SIDE for d in range(SIDE)][1:]
    rows_at[0] = y * SIDE
    cols_at = [x] + [wrap(x + d) for d in range(1, SIDE)]
    chips = [rows_at[dy] + cols_at[dx] for dy, dx in ROUTE]
    deep = [z] + [wrap(z + d) for d in range(1, DEPTH)]
    mates = [(core if k < DEPTH else 1 - core, deep[k % DEPTH]) for k in range(1, 2 * DEPTH)]

    for b in range(SAMPLES):
        pltpu.make_async_copy(og_hbm.at[b], og.at[b], og_sem.at[b]).start()
        pltpu.make_async_copy(act_hbm.at[b], act.at[b], load_sem.at[b]).start()

    barrier = pltpu.get_barrier_semaphore()
    everyone = [
        (rows_at[dy] * 2 + cols_at[dx] * 2 + (1 - core if dc else core), deep[dz]) for dy, dx, dc, dz in EVERYONE
    ]
    for q in chips:
        for half in range(2):
            pl.semaphore_signal(barrier, inc=1, device_id={"dp": q * 2 + half}, device_id_type=MESH)
    for c2, z2 in mates:
        pl.semaphore_signal(barrier, inc=1, device_id={"dp": chip * 2 + c2, "chan": z2}, device_id_type=MESH)

    def remote(src, dst, send, recv, dp_to, z_to=None):
        to = {"dp": dp_to} if z_to is None else {"dp": dp_to, "chan": z_to}
        return pltpu.make_async_remote_copy(
            src_ref=src, dst_ref=dst, send_sem=send, recv_sem=recv, device_id=to, device_id_type=MESH
        )

    def landed(ref, sem):
        pltpu.make_async_copy(ref, ref, sem).wait()

    for j in range(3):
        for b in range(SAMPLES):
            pad[j, b, :32] = jnp.zeros((32, LANES), pad.dtype)
            pad[j, b, 32 + SPACE :] = jnp.zeros((32, LANES), pad.dtype)

    def columns(b, taps):
        return jnp.concatenate(
            [pad[t % 3, b, (2 - t // 3) * 32 : (2 - t // 3) * 32 + SPACE, :] for t in taps], axis=1
        )

    def store(grad, product, first):
        for t in range(product.shape[1] // LANES):
            tap = product[:, t * LANES : (t + 1) * LANES].reshape(CHIPS, 2, ROWS, LANES)
            for half in range(2):
                if first:
                    grad[half, :, t] = tap[:, half]
                else:
                    grad[half, :, t] += tap[:, half]

    def product(left, right):
        return lax.dot_general(left, right, (((0,), (0,)), ((), ())), preferred_element_type=F32)

    def move(b):
        for j, moved in enumerate(shifted(og[b])):
            pad[j, b, 32 : 32 + SPACE, :] = moved

    def early(b, carry, first=False, last=False):
        landed(act.at[b], load_sem.at[b])
        if not last:
            landed(og.at[b + 1], og_sem.at[b + 1])
        store(grad_a, product(act[b], columns(b, range(EARLY))), first)
        if not last:
            move(b + 1)
        return carry

    def later(grad, taps, span):
        def body(k, carry, first=False):
            left = act[pl.ds(span * k, span)].reshape(span * SPACE, CIN)
            right = jnp.concatenate([columns(span * k + n, taps) for n in range(span)], axis=0)
            store(grad, product(left, right), first)
            return carry

        body(0, 0, True)
        lax.fori_loop(1, SAMPLES // span, body, 0)

    landed(og.at[0], og_sem.at[0])
    move(0)
    early(0, 0, first=True)
    lax.fori_loop(1, SAMPLES - 1, early, 0)
    early(SAMPLES - 1, 0, last=True)

    pl.semaphore_wait(barrier, 2 * (CHIPS - 1) + 2 * DEPTH - 1)

    def swap(n, grad, sib):
        copy = remote(grad.at[1 - core], sib, sib_send.at[n], sib_recv.at[n], chip * 2 + 1 - core)
        copy.start()
        return copy

    swaps = [swap(0, grad_a, sib_a)]
    for q in chips:
        for half in range(2):
            remote(
                grad_a.at[half, q], raw_a.at[core, chip], raw_send.at[half], raw_recv.at[core], q * 2 + half
            ).start()

    later(grad_b, range(EARLY, MIDDLE), 2)
    swaps.append(swap(1, grad_b, sib_b))
    for q in chips:
        for half in range(2):
            remote(
                grad_b.at[half, q, : RAW - EARLY],
                raw_b.at[core, chip],
                raw_send.at[2 + half],
                raw_recv.at[2 + core],
                q * 2 + half,
            ).start()
    later(grad_c, range(MIDDLE, TAPS), 4)
    swaps.append(swap(2, grad_c, sib_c))

    def products(grad, sib, sums):
        def body(q, carry):
            mine = grad[core, q]
            theirs = sib[q]
            return (
                carry[0] + fold(mine * theirs),
                carry[1] + fold(mine * mine),
                carry[2] + fold(theirs * theirs),
            )

        return lax.fori_loop(0, CHIPS, body, sums, unroll=8)

    zero = jnp.zeros((8, LANES), F32)
    sums = (zero, zero, zero)
    for copy, grad, sib in zip(swaps, (grad_a, grad_b, grad_c), (sib_a, sib_b, sib_c)):
        copy.wait_recv()
        sums = products(grad, sib, sums)
    scal_src[0] = sums[0]
    scal_src[1] = jnp.where(core == 0, sums[1], sums[2])
    scal_src[2] = jnp.where(core == 0, sums[2], sums[1])
    for c2, z2 in mates:
        remote(scal_src, scal.at[slot], scal_send.at[0], scal_recv.at[0], chip * 2 + c2, z2).start()
    scal[slot] = scal_src[...]
    landed(scal.at[: 2 * DEPTH - 1], scal_recv.at[0])
    added = jnp.sum(scal[...], axis=0)
    inner, low_sq, high_sq = total(added[0]), total(added[1]), total(added[2])
    low = 1.0 - inner / (2.0 * (low_sq + EPS))
    high = 1.0 - inner / (2.0 * (high_sq + EPS))
    coef_src[0:1] = jnp.broadcast_to(low, (1, LANES))
    coef_src[1:2] = jnp.broadcast_to(high, (1, LANES))
    my_coef = jnp.where(core == 0, low, high)
    their_coef = jnp.where(core == 0, high, low)

    skip = RAW - EARLY

    def mixed(mine, theirs):
        return my_coef * mine + their_coef * theirs

    for k, q in enumerate(chips):
        remote(coef_src, coef.at[chip], coef_send.at[0], coef_recv.at[0], q * 2 + core).start()
        comb_b[k] = mixed(grad_b[core, q, skip:], sib_b[q, skip:])
        remote(comb_b.at[k], block_b.at[chip], comb_send.at[0], comb_recv.at[0], q * 2 + core).start()
    for k, q in enumerate(chips):
        comb_c[k] = mixed(grad_c[core, q], sib_c[q])
        remote(comb_c.at[k], block_c.at[chip], comb_send.at[1], comb_recv.at[1], q * 2 + core).start()
    block_b[chip] = mixed(grad_b[core, chip, skip:], sib_b[chip, skip:])
    block_c[chip] = mixed(grad_c[core, chip], sib_c[chip])
    block_a[chip, :EARLY] = my_coef * grad_a[core, chip] + their_coef * sib_a[chip]
    block_a[chip, EARLY:] = my_coef * grad_b[core, chip, :skip] + their_coef * sib_b[chip, :skip]
    for half in range(2):
        landed(raw_a.at[half, : CHIPS - 1], raw_recv.at[half])
        landed(raw_b.at[half, : CHIPS - 1], raw_recv.at[2 + half])
    landed(coef.at[: CHIPS - 1], coef_recv.at[0])
    for q in chips:
        block_a[q, :EARLY] = coef[q, 0:1] * raw_a[0, q] + coef[q, 1:2] * raw_a[1, q]
        block_a[q, EARLY:] = coef[q, 0:1] * raw_b[0, q] + coef[q, 1:2] * raw_b[1, q]

    def against(block, more):
        def body(s, carry):
            mine = block[s]
            for t in range(CHIPS):
                part = fold(mine * block[t])
                pairs[s, t] = part + pairs[s, t] if more else part
            return carry

        lax.fori_loop(0, CHIPS, body, 0)

    against(block_a, False)
    landed(block_b.at[: CHIPS - 1], comb_recv.at[0])
    against(block_b, True)
    landed(block_c.at[: CHIPS - 1], comb_recv.at[1])
    against(block_c, True)

    sums = jnp.sum(jnp.sum(pairs[...].reshape(CHIPS * CHIPS, 8, LANES), axis=1), axis=1, keepdims=True)
    index = lax.broadcasted_iota(jnp.int32, (CHIPS * CHIPS, LANES), 0)
    lane = lax.broadcasted_iota(jnp.int32, (CHIPS * CHIPS, LANES), 1)
    spread = jnp.where(lane == index % (CHIPS * PACKED), sums, 0.0)
    gram_src[...] = jnp.sum(spread.reshape(2, CHIPS * PACKED, LANES), axis=1)

    here = dp * DEPTH + z
    for device, level in everyone:
        remote(gram_src, gram_all.at[here], gram_send.at[0], gram_recv.at[0], device, level).start()
    gram_all[here] = gram_src[...]
    for copy in swaps:
        copy.wait_send()
    for half in range(2):
        landed(raw_a.at[half, : CHIPS - 1], raw_send.at[half])
        landed(raw_b.at[half, : CHIPS - 1], raw_send.at[2 + half])
    landed(scal.at[: 2 * DEPTH - 1], scal_send.at[0])
    landed(coef.at[: CHIPS - 1], coef_send.at[0])
    landed(comb_b, comb_send.at[0])
    landed(comb_c, comb_send.at[1])
    landed(gram_all.at[: DEVICES - 1], gram_recv.at[0])
    packed = jnp.sum(gram_all[...], axis=0)
    rows = jnp.concatenate([jnp.broadcast_to(packed[n : n + 1], (PACKED, LANES)) for n in range(2)], axis=0)
    row = lax.broadcasted_iota(jnp.int32, (CHIPS, LANES), 0) % PACKED
    gram = rows
    for n in range(1, PACKED):
        gram = jnp.where(row == n, pltpu.roll(rows, LANES - CHIPS * n, 1), gram)
    gram = jnp.where(lax.broadcasted_iota(jnp.int32, (CHIPS, LANES), 1) < CHIPS, gram, 0.0)
    weights = pair_weights(gram)

    for t in range(TAPS):
        block, u = (block_a, t) if t < RAW else (block_b, t - RAW) if t < MIDDLE else (block_c, t - MIDDLE)
        tap = weights[0:1] * block[0, u]
        for s in range(1, CHIPS):
            tap = tap + weights[s : s + 1] * block[s, u]
        out_ref[t] = tap
    landed(gram_all.at[: DEVICES - 1], gram_send.at[0])


def adasum(activations, out_grads):
    bf16 = jnp.bfloat16
    scratch = [
        pltpu.VMEM((SAMPLES, SPACE, CIN), bf16),
        pltpu.VMEM((SAMPLES, SPACE, LANES), bf16),
        pltpu.VMEM((3, SAMPLES, SPACE + 64, LANES), bf16),
    ]
    scratch += [
        pltpu.VMEM(shape, F32)
        for shape in (
            (2, CHIPS, EARLY, ROWS, LANES),
            (2, CHIPS, MIDDLE - EARLY, ROWS, LANES),
            (2, CHIPS, TAPS - MIDDLE, ROWS, LANES),
            (CHIPS, EARLY, ROWS, LANES),
            (CHIPS, MIDDLE - EARLY, ROWS, LANES),
            (CHIPS, TAPS - MIDDLE, ROWS, LANES),
            (2, CHIPS, EARLY, ROWS, LANES),
            (2, CHIPS, RAW - EARLY, ROWS, LANES),
            (CHIPS - 1, MIDDLE - RAW, ROWS, LANES),
            (CHIPS - 1, TAPS - MIDDLE, ROWS, LANES),
            (CHIPS, RAW, ROWS, LANES),
            (CHIPS, MIDDLE - RAW, ROWS, LANES),
            (CHIPS, TAPS - MIDDLE, ROWS, LANES),
            (3, 8, LANES),
            (2 * DEPTH, 3, 8, LANES),
            (2, LANES),
            (CHIPS, 2, LANES),
            (CHIPS, CHIPS, 8, LANES),
            (2, LANES),
            (DEVICES, 2, LANES),
        )
    ]
    scratch += [
        pltpu.SemaphoreType.DMA(shape)
        for shape in (
            (SAMPLES,), (SAMPLES,), (3,), (3,), (4,), (4,), (1,), (1,), (1,), (1,), (2,), (2,), (1,), (1,),
        )
    ]
    return pl.pallas_call(
        kernel,
        out_shape=jax.ShapeDtypeStruct((9, ROWS, LANES), F32),
        in_specs=[pl.BlockSpec(memory_space=pltpu.HBM)] * 2,
        out_specs=pl.BlockSpec(memory_space=pltpu.VMEM),
        scratch_shapes=scratch,
        compiler_params=pltpu.CompilerParams(
            collective_id=0, has_side_effects=True, vmem_limit_bytes=52 << 20
        ),
        name="adasum",
    )(activations.reshape(SAMPLES, SPACE, CIN), out_grads.reshape(SAMPLES, SPACE, LANES))


def shards(activations, out_grads, weight, momentum):
    combined = adasum(activations, out_grads)
    combined = combined.transpose(1, 0, 2).reshape(weight.shape)
    new_momentum = 0.9 * momentum + combined
    new_weight = weight - 0.1 * new_momentum
    return new_weight, new_momentum


def solution(mesh):
    in_specs = (
        P("dp", None, None, None),
        P("dp", None, None, "chan"),
        P("dp", None, None, "chan"),
        P("dp", None, None, "chan"),
    )
    out_specs = (P("dp", None, None, "chan"), P("dp", None, None, "chan"))
    return jax.shard_map(shards, mesh=mesh, in_specs=in_specs, out_specs=out_specs, check_vma=False)
```
